32 devices in a mesh: dp: 16 (over z, y, core), tp: 2 (over x).
Axes of the slice: x: 2, y: 2, z: 4, core: 2. Of those that a mesh axis runs over, the one named last changes fastest.
Arguments:
- tokens: bfloat16 [16384, 768], P(('dp', 'tp')), may hold values from -6 to 6
- segment_ids: int32 [16384], P('dp'), may hold values from 0 to 63, never falling along the last dimension, each value on 1 to 512 neighbouring positions
- first_gain: float32 [768], replicated, may hold values from 0.5 to 1.5
- first_shift: float32 [768], replicated, may hold values from -1.75 to 1.75
- qkv_weight: bfloat16 [768, 3, 768], P(None, None, 'tp'), may hold values from -0.21875 to 0.21875
- query_bias: float32 [768], P('tp'), may hold values from -3 to 3
- value_bias: float32 [768], P('tp'), may hold values from -3 to 3
- out_weight: bfloat16 [768, 768], P('tp'), may hold values from -0.875 to 0.875
- out_bias: float32 [768], replicated, may hold values from -1.75 to 1.75
- second_gain: float32 [768], replicated, may hold values from 0.5 to 1.5
- second_shift: float32 [768], replicated, may hold values from -1.75 to 1.75
- up_weight: bfloat16 [768, 3072], P(None, 'tp'), may hold values from -0.21875 to 0.21875
- up_bias: float32 [3072], P('tp'), may hold values from -3 to 3
- down_weight: bfloat16 [3072, 768], P('tp'), may hold values from -0.109375 to 0.109375
- down_bias: float32 [768], replicated, may hold values from -1.75 to 1.75
- grad_out: bfloat16 [16384, 768], P(('dp', 'tp')), may hold values from -6 to 6
Outputs:
- layer_out: bfloat16 [16384, 768], P(('dp', 'tp'))
- tokens_grad: bfloat16 [16384, 768], P(('dp', 'tp'))
- first_gain_grad: float32 [768], replicated
- first_shift_grad: float32 [768], replicated
- qkv_grad: float32 [768, 3, 768], P(None, None, 'tp')
- query_bias_grad: float32 [768], P('tp')
- value_bias_grad: float32 [768], P('tp')
- out_weight_grad: float32 [768, 768], P('tp')
- out_bias_grad: float32 [768], replicated
- second_gain_grad: float32 [768], replicated
- second_shift_grad: float32 [768], replicated
- up_weight_grad: float32 [768, 3072], P(None, 'tp')
- up_bias_grad: float32 [3072], P('tp')
- down_weight_grad: float32 [3072, 768], P('tp')
- down_bias_grad: float32 [768], replicated
The draws below stay inside these ranges and needn't reach their ends.
Inputs may be any that keep to these rules, and one draw needn't show every extreme that they name: `segment_ids`: segment numbers never fall along the patches; each segment holds 1 to 512 patches, one exactly 512.
All inputs are finite; a program needn't handle non-finite values.
Results may differ from the reference program's by a relative error of at most 0.018.
Values may be sent and summed in bfloat16 or wider, within the bound.
No kernel may reach another device: no remote copies, remote signals or barrier semaphores. Data moves between devices by JAX's collectives and lax.ppermute only.
A program may use at most 192 MiB of HBM per device.

```python
import math
import jax
import jax.numpy as jnp
import numpy as np
from jax import lax

D = 768
HEADS = 12
HEAD = 64
FF = 3072
PACK = 1024
TOKENS = 16384
SEGMENTS = 64
N_DP = 16


def level_of(stream_key, shape, split, smallest, largest):
    def one(axis_at, parts):
        draws = jax.random.uniform(jax.random.fold_in(jax.random.fold_in(stream_key, 6), axis_at), (parts,), jnp.float32, smallest / len(split), largest / len(split))
        return jnp.repeat(jnp.exp(draws), shape[axis_at] // parts).reshape((-1,) + (1,) * (len(shape) - axis_at - 1))

    level = one(*split[0])
    for cut in split[1:]:
        level = level * one(*cut)
    return level


def split_up(amount, total, most, slope):
    loads = [(1 << 20) // math.isqrt(grade ** slope) + 1 for grade in range(2, amount + 1)]
    rest, counts = total - most - (amount - 1), [1] * (amount - 1)
    while rest > 0:
        free = [i for i in range(amount - 1) if counts[i] < most]
        whole, left = sum([loads[i] for i in free]), rest
        for i in free:
            more = min(most - counts[i], max(1, left * loads[i] // whole), rest)
            counts[i] = counts[i] + more
            rest = rest - more
    return np.array([most] + counts)


def ragged(stream_key, number_of, total, bound, skew):
    if number_of == 2:
        one = jax.random.randint(stream_key, (), max(1, total - bound), min(bound, total - 1) + 1)
        return jnp.stack([one, total - one])
    tallies = jnp.asarray(split_up(number_of, total, bound, skew), jnp.int32)
    twos = (number_of - 1) // 2
    donor, sink = tallies[1:1 + 2 * twos:2], tallies[2:2 + 2 * twos:2]
    room = jnp.minimum(donor - 1, bound - sink)
    moved = jax.random.randint(jax.random.fold_in(stream_key, 1), (twos,), 0, 1 << 20) % (room + 1)
    tallies = tallies.at[1:1 + 2 * twos:2].set(donor - moved).at[2:2 + 2 * twos:2].set(sink + moved)
    return tallies[jax.random.permutation(jax.random.fold_in(stream_key, 2), number_of)]


def bell_draw(own_key, dims, scale, most, cuts=(), dtype=jnp.bfloat16):
    array = jax.random.normal(own_key, dims, jnp.float32) * scale
    if len(cuts) > 0:
        array = level_of(own_key, dims, cuts, -0.22, 0.18) * array
    return jnp.clip(array, min=-most, max=most).astype(dtype)


def setup_inputs(seed: int = 0) -> dict:
    splits = jax.random.split(jax.random.key(seed), 17)
    tokens = bell_draw(splits[0], (TOKENS, D), 1.0, 6.0, ((0, 32),))
    segment_ids = jnp.searchsorted(jnp.cumsum(ragged(splits[1], SEGMENTS, TOKENS, PACK // 2, 1)), jnp.arange(TOKENS), side="right").astype(jnp.int32)
    first_gain = jnp.clip(1.0 + 0.1 * jax.random.normal(splits[2], (D,), jnp.float32), 0.5, 1.5)
    first_shift = bell_draw(splits[3], (D,), 0.3, 1.75, (), jnp.float32)
    qkv_weight = bell_draw(splits[4], (D, 3, D), D ** -0.5, 0.21875, ((2, 2),))
    query_bias = bell_draw(splits[5], (D,), 0.5, 3.0, ((0, 2),), jnp.float32)
    value_bias = bell_draw(splits[6], (D,), 0.5, 3.0, ((0, 2),), jnp.float32)
    out_weight = bell_draw(splits[7], (D, D), (D // 16) ** -0.5, 0.875, ((0, 2),))
    out_bias = bell_draw(splits[8], (D,), 0.3, 1.75, (), jnp.float32)
    second_gain = jnp.clip(1.0 + 0.1 * jax.random.normal(splits[9], (D,), jnp.float32), 0.5, 1.5)
    second_shift = bell_draw(splits[10], (D,), 0.3, 1.75, (), jnp.float32)
    up_weight = bell_draw(splits[11], (D, FF), D ** -0.5, 0.21875, ((1, 2),))
    up_bias = bell_draw(splits[12], (FF,), 0.5, 3.0, ((0, 2),), jnp.float32)
    down_weight = bell_draw(splits[13], (FF, D), FF ** -0.5, 0.109375, ((0, 2),))
    down_bias = bell_draw(splits[14], (D,), 0.3, 1.75, (), jnp.float32)
    grad_out = bell_draw(splits[15], (TOKENS, D), 1.0, 6.0, ((0, 32),))
    return {"tokens": tokens, "segment_ids": segment_ids, "first_gain": first_gain, "first_shift": first_shift, "qkv_weight": qkv_weight, "query_bias": query_bias, "value_bias": value_bias, "out_weight": out_weight, "out_bias": out_bias, "second_gain": second_gain, "second_shift": second_shift, "up_weight": up_weight, "up_bias": up_bias, "down_weight": down_weight, "down_bias": down_bias, "grad_out": grad_out}


@jax.custom_vjp
def low(v):
    return lax.optimization_barrier(v.astype(jnp.bfloat16)).astype(jnp.float32)

@jax.custom_vjp
def low_back(v):
    return v

def low_keep(v):
    return (low(v), None)

def low_pass(kept, grad):
    return (grad,)

def back_keep(v):
    return (v, None)

def back_low(kept, grad):
    return (low(grad),)
low.defvjp(low_keep, low_pass)
low_back.defvjp(back_keep, back_low)
EPS = 1e-06
HIGH = lax.Precision.HIGHEST

def normalize(values, gain, shift):
    center = values - lax.optimization_barrier(jnp.mean(values, axis=-1, keepdims=True))
    spread = lax.optimization_barrier(jnp.mean(center * center, axis=-1, keepdims=True))
    return center * lax.rsqrt(spread + EPS) * gain + shift

def matmul(left, right):
    return jnp.dot(left, right, precision=HIGH)

def forward(inputs, segments, params):
    gain_one, shift_one, qkv_w, q_bias, v_bias, out_w, o_bias, gain_two, shift_two, up_w, u_bias, down_w, d_bias = params
    count = inputs.shape[0]
    first_low = low(normalize(inputs, gain_one, shift_one))
    projected = low_back(matmul(first_low, qkv_w.reshape(D, 3 * D))).reshape(count, 3, HEADS, HEAD)
    queries = low(projected[:, 0] + q_bias.reshape(HEADS, HEAD))
    keys_all = low(projected[:, 1])
    values_all = low(projected[:, 2] + v_bias.reshape(HEADS, HEAD))
    scores = low_back(jnp.einsum('qhd,khd->hqk', queries, keys_all, precision=HIGH) * HEAD ** (-0.5))
    same_doc = segments[:, None] == segments[None, :]
    scores = jnp.where(same_doc[None], scores, -1e+30)
    probs_low = low(jax.nn.softmax(scores, axis=-1))
    attended = low_back(low(jnp.einsum('hqk,khd->qhd', probs_low, values_all, precision=HIGH))).reshape(count, D)
    middle = inputs + low_back(matmul(attended, out_w)) + o_bias
    second_low = low(normalize(middle, gain_two, shift_two))
    pre_act = low_back(matmul(second_low, up_w)) + u_bias
    hidden = low(jax.nn.gelu(pre_act, approximate=False))
    return middle + low_back(matmul(hidden, down_w)) + d_bias

def reference(tokens, segment_ids, first_gain, first_shift, qkv_weight, query_bias, value_bias, out_weight, out_bias, second_gain, second_shift, up_weight, up_bias, down_weight, down_bias, grad_out):
    params = tuple((item.astype(jnp.float32) for item in (first_gain, first_shift, qkv_weight, query_bias, value_bias, out_weight, out_bias, second_gain, second_shift, up_weight, up_bias, down_weight, down_bias)))
    inputs = tokens.astype(jnp.float32).reshape(N_DP, PACK, D)
    cotangents = grad_out.astype(jnp.float32).reshape(N_DP, PACK, D)
    segments = segment_ids.reshape(N_DP, PACK)

    def step(running, item):
        row_in, row_seg, row_cot = item
        row_out, pull = jax.vjp(lambda value_in, value_params: forward(value_in, row_seg, value_params), row_in, params)
        row_grad, param_grads = pull(row_cot)
        running = jax.tree.map(jnp.add, running, param_grads)
        return (running, (row_out.astype(jnp.bfloat16), row_grad.astype(jnp.bfloat16)))
    zeros = jax.tree.map(jnp.zeros_like, params)
    totals, (outputs, grads) = lax.scan(step, zeros, (inputs, segments, cotangents))
    return (outputs.reshape(TOKENS, D), grads.reshape(TOKENS, D), totals[0], totals[1], totals[2], totals[3], totals[4], totals[5], totals[6], totals[7], totals[8], totals[9], totals[10], totals[11], totals[12])
```

```python
import jax
import jax.numpy as jnp
from jax import lax
from jax.experimental import pallas as pl
from jax.experimental.pallas import tpu as pltpu
from jax.sharding import PartitionSpec as P

HEAD = 64
EPS = 1e-06
MASKED = -1e30
BLK = 256
PAIR = 2 * HEAD
f32 = jnp.float32
bf16 = jnp.bfloat16


def stats(values):
    center = values - jnp.mean(values, axis=-1, keepdims=True)
    spread = jnp.mean(center * center, axis=-1, keepdims=True)
    scale = lax.rsqrt(spread + EPS)
    return center * scale, scale


def dot_nt(left, right):
    return lax.dot_general(left, right, (((1,), (1,)), ((), ())), preferred_element_type=f32)


def dot_nn(left, right):
    return lax.dot_general(left, right, (((1,), (0,)), ((), ())), preferred_element_type=f32)


def dot_tn(left, right):
    return lax.dot_general(left, right, (((0,), (0,)), ((), ())), preferred_element_type=f32)


def meets(lo_ref, hi_ref, i, j):
    return (lo_ref[j] <= hi_ref[i]) & (hi_ref[j] >= lo_ref[i])


def by_head(block):
    lane = lax.broadcasted_iota(jnp.int32, block.shape, 1)
    zero = jnp.zeros_like(block)
    return jnp.where(lane < HEAD, block, zero), jnp.where(lane < HEAD, zero, block)


def attend_kernel(lo_ref, hi_ref, q_ref, k_ref, v_ref, row_ref, col_ref, out_ref, lse_ref, vt_ref, acc_ref, m_ref, l_ref):
    i = pl.program_id(1)
    blocks = k_ref.shape[0] // BLK

    @pl.when(i == 0)
    def _():
        vt_ref[...] = v_ref[...].T

    acc_ref[...] = jnp.zeros_like(acc_ref)
    m_ref[...] = jnp.full_like(m_ref, MASKED)
    l_ref[...] = jnp.zeros_like(l_ref)
    queries = by_head(q_ref[...])
    row_seg = row_ref[0:1, :]

    def step(j, carry):
        @pl.when(meets(lo_ref, hi_ref, i, j))
        def _():
            at = pl.multiple_of(j * BLK, BLK)
            keys = k_ref[pl.ds(at, BLK), :]
            col = col_ref[pl.ds(at, BLK), :]
            same = jnp.concatenate([col] * (BLK // 128), axis=1) == row_seg
            for h in range(2):
                scores = jnp.where(same, dot_nt(keys, queries[h]), MASKED)
                old = m_ref[h : h + 1, :]
                new = jnp.maximum(old, jnp.max(scores, axis=0, keepdims=True))
                fade = jnp.exp(old - new)
                expon = jnp.where(same, jnp.exp(scores - new), 0.0)
                m_ref[h : h + 1, :] = new
                l_ref[h : h + 1, :] = fade * l_ref[h : h + 1, :] + jnp.sum(expon, axis=0, keepdims=True)
                span = slice(h * HEAD, (h + 1) * HEAD)
                acc_ref[span, :] = fade * acc_ref[span, :] + dot_nn(
                    vt_ref[span, pl.ds(at, BLK)], expon.astype(bf16)
                )

        return carry

    lax.fori_loop(0, blocks, step, 0)
    halves = [acc_ref[h * HEAD : (h + 1) * HEAD, :] / l_ref[h : h + 1, :] for h in range(2)]
    out_ref[...] = jnp.concatenate(halves, axis=0).T.astype(bf16)
    lse_ref[...] = jnp.concatenate(
        [m_ref[0:2, :] + jnp.log(l_ref[0:2, :]), jnp.zeros((6, BLK), f32)], axis=0
    )


def attend(qkv, lo, hi, seg_row, seg_col, pairs):
    rows = qkv.shape[0]
    return pl.pallas_call(
        attend_kernel,
        grid_spec=pltpu.PrefetchScalarGridSpec(
            num_scalar_prefetch=2,
            grid=(pairs, rows // BLK),
            in_specs=[
                pl.BlockSpec((BLK, PAIR), lambda p, i, *_: (i, p)),
                pl.BlockSpec((rows, PAIR), lambda p, i, *_: (0, pairs + p)),
                pl.BlockSpec((rows, PAIR), lambda p, i, *_: (0, 2 * pairs + p)),
                pl.BlockSpec((8, BLK), lambda p, i, *_: (0, i)),
                pl.BlockSpec((rows, 128), lambda p, i, *_: (0, 0)),
            ],
            out_specs=[
                pl.BlockSpec((BLK, PAIR), lambda p, i, *_: (i, p)),
                pl.BlockSpec((8, BLK), lambda p, i, *_: (p, i)),
            ],
            scratch_shapes=[
                pltpu.VMEM((PAIR, rows), bf16),
                pltpu.VMEM((PAIR, BLK), f32),
                pltpu.VMEM((8, BLK), f32),
                pltpu.VMEM((8, BLK), f32),
            ],
        ),
        out_shape=[
            jax.ShapeDtypeStruct((rows, pairs * PAIR), bf16),
            jax.ShapeDtypeStruct((8 * pairs, rows), f32),
        ],
        name="attend",
    )(lo, hi, qkv, qkv, qkv, seg_row, seg_col)


def attend_back_kernel(
    lo_ref, hi_ref, q_ref, k_ref, v_ref, g_ref, o_ref, lse_ref, row_ref, col_ref,
    dq_ref, dk_ref, dv_ref, qb_ref, vb_ref, kt_ref, dk_acc, dv_acc, dq_acc,
):
    i = pl.program_id(1)
    blocks = k_ref.shape[0] // BLK

    @pl.when(i == 0)
    def _():
        kt_ref[...] = k_ref[...].T
        dk_acc[...] = jnp.zeros_like(dk_acc)
        dv_acc[...] = jnp.zeros_like(dv_acc)
        qb_ref[...] = jnp.zeros_like(qb_ref)

    dq_acc[...] = jnp.zeros_like(dq_acc)
    queries = by_head(q_ref[...])
    grads = by_head(g_ref[...])
    prod = (g_ref[...].astype(f32) * o_ref[...].astype(f32)).T
    inner = [jnp.sum(prod[h * HEAD : (h + 1) * HEAD], axis=0, keepdims=True) for h in range(2)]
    row_seg = row_ref[0:1, :]

    def step(j, carry):
        @pl.when(meets(lo_ref, hi_ref, i, j))
        def _():
            at = pl.multiple_of(j * BLK, BLK)
            keys = k_ref[pl.ds(at, BLK), :]
            vals = v_ref[pl.ds(at, BLK), :]
            col = col_ref[pl.ds(at, BLK), :]
            same = jnp.concatenate([col] * (BLK // 128), axis=1) == row_seg
            dv_new = dv_acc[pl.ds(at, BLK), :]
            dk_new = dk_acc[pl.ds(at, BLK), :]
            for h in range(2):
                scores = jnp.where(same, dot_nt(keys, queries[h]), MASKED)
                probs = jnp.exp(scores - lse_ref[h : h + 1, :])
                dv_new = dv_new + dot_nn(probs.astype(bf16), grads[h])
                back = (probs * (dot_nt(vals, grads[h]) - inner[h])).astype(bf16)
                dk_new = dk_new + dot_nn(back, queries[h])
                span = slice(h * HEAD, (h + 1) * HEAD)
                dq_acc[span, :] += dot_nn(kt_ref[span, pl.ds(at, BLK)], back)
            dv_acc[pl.ds(at, BLK), :] = dv_new
            dk_acc[pl.ds(at, BLK), :] = dk_new

        return carry

    lax.fori_loop(0, blocks, step, 0)
    dq = dq_acc[...].T * HEAD ** (-0.5)
    dq_ref[...] = dq.astype(bf16)
    qb_ref[0:1, :] += jnp.sum(dq, axis=0, keepdims=True)

    @pl.when(i == pl.num_programs(1) - 1)
    def _():
        dk_ref[...] = dk_acc[...].astype(bf16)
        dv = dv_acc[...]
        dv_ref[...] = dv.astype(bf16)
        vb_ref[...] = jnp.broadcast_to(jnp.sum(dv, axis=0, keepdims=True), vb_ref.shape)


def attend_back(qkv, grads, attended, lse, lo, hi, seg_row, seg_col, pairs):
    rows = qkv.shape[0]
    wide = pairs * PAIR
    return pl.pallas_call(
        attend_back_kernel,
        grid_spec=pltpu.PrefetchScalarGridSpec(
            num_scalar_prefetch=2,
            grid=(pairs, rows // BLK),
            in_specs=[
                pl.BlockSpec((BLK, PAIR), lambda p, i, *_: (i, p)),
                pl.BlockSpec((rows, PAIR), lambda p, i, *_: (0, pairs + p)),
                pl.BlockSpec((rows, PAIR), lambda p, i, *_: (0, 2 * pairs + p)),
                pl.BlockSpec((BLK, PAIR), lambda p, i, *_: (i, p)),
                pl.BlockSpec((BLK, PAIR), lambda p, i, *_: (i, p)),
                pl.BlockSpec((8, BLK), lambda p, i, *_: (p, i)),
                pl.BlockSpec((8, BLK), lambda p, i, *_: (0, i)),
                pl.BlockSpec((rows, 128), lambda p, i, *_: (0, 0)),
            ],
            out_specs=[
                pl.BlockSpec((BLK, PAIR), lambda p, i, *_: (i, p)),
                pl.BlockSpec((rows, PAIR), lambda p, i, *_: (0, p)),
                pl.BlockSpec((rows, PAIR), lambda p, i, *_: (0, p)),
                pl.BlockSpec((8, PAIR), lambda p, i, *_: (0, p)),
                pl.BlockSpec((8, PAIR), lambda p, i, *_: (0, p)),
            ],
            scratch_shapes=[
                pltpu.VMEM((PAIR, rows), bf16),
                pltpu.VMEM((rows, PAIR), f32),
                pltpu.VMEM((rows, PAIR), f32),
                pltpu.VMEM((PAIR, BLK), f32),
            ],
        ),
        out_shape=[
            jax.ShapeDtypeStruct((rows, wide), bf16),
            jax.ShapeDtypeStruct((rows, wide), bf16),
            jax.ShapeDtypeStruct((rows, wide), bf16),
            jax.ShapeDtypeStruct((8, wide), f32),
            jax.ShapeDtypeStruct((8, wide), f32),
        ],
        name="attend_back",
    )(lo, hi, qkv, qkv, qkv, grads, attended, lse, seg_row, seg_col)


def make(n_dp):
    bits = n_dp.bit_length() - 1

    def swap_tp(value):
        return lax.ppermute(value, "tp", [(0, 1), (1, 0)])

    def swap_dp(value, bit):
        return lax.ppermute(value, "dp", [(d, d ^ (1 << bit)) for d in range(n_dp)])

    def reduce_dp(value, order):
        spot = lax.axis_index("dp")
        for bit in order:
            half = value.shape[0] // 2
            mine = (spot >> bit) & 1
            sent = lax.dynamic_slice_in_dim(value, (1 - mine) * half, half, 0)
            kept = lax.dynamic_slice_in_dim(value, mine * half, half, 0)
            value = (kept.astype(f32) + swap_dp(sent, bit).astype(f32)).astype(bf16)
        for bit in reversed(order):
            mine = ((spot >> bit) & 1) == 0
            came = swap_dp(value, bit)
            value = jnp.concatenate(
                [jnp.where(mine, value, came), jnp.where(mine, came, value)], axis=0
            )
        return value

    def small_sum(value, with_tp):
        if with_tp:
            value = value + swap_tp(value)
        for bit in range(bits):
            value = value + swap_dp(value, bit)
        return value

    order = list(range(bits))

    def on_device(
        tokens, segment_ids, first_gain, first_shift, qkv_weight, query_bias, value_bias, out_weight,
        out_bias, second_gain, second_shift, up_weight, up_bias, down_weight, down_bias, grad_out,
    ):
        width = tokens.shape[1]
        local = qkv_weight.shape[2]
        rows = segment_ids.shape[0]
        own = rows // 2
        pairs = local // PAIR
        qkv_flat = qkv_weight.reshape(width, 3 * local)

        def other(value):
            return swap_tp(value)

        tokens_all = jnp.concatenate([tokens, other(tokens)], axis=0)
        grad_all = jnp.concatenate([grad_out, other(grad_out)], axis=0)
        here = lax.axis_index("tp")
        segs = jnp.where(here == 0, segment_ids, jnp.roll(segment_ids, own))
        seg_row = jnp.broadcast_to(segs[None, :], (8, rows))
        seg_col = jnp.broadcast_to(segs[:, None], (rows, 128))
        blocked = segs.reshape(rows // BLK, BLK)
        lo, hi = blocked[:, 0], blocked[:, BLK - 1]

        first_z, first_scale = stats(tokens_all.astype(f32))
        first_low = (first_z * first_gain + first_shift).astype(bf16)
        bias = jnp.concatenate([query_bias, jnp.zeros_like(query_bias), value_bias])
        size = jnp.concatenate([jnp.full((local,), HEAD ** (-0.5), f32), jnp.ones((2 * local,), f32)])
        qkv = ((dot_nn(first_low, qkv_flat) + bias) * size).astype(bf16)
        attended, lse = attend(qkv, lo, hi, seg_row, seg_col, pairs)
        out_there = dot_nn(attended[own:], out_weight).astype(bf16)
        out_here = dot_nn(attended[:own], out_weight)
        middle = tokens.astype(f32) + (out_here + other(out_there).astype(f32)) + out_bias
        second_z, second_scale = stats(middle)
        second_own = (second_z * second_gain + second_shift).astype(bf16)
        second_low = jnp.concatenate([second_own, other(second_own)], axis=0)
        pre_act = dot_nn(second_low, up_weight) + up_bias
        below = 0.5 * (1.0 + lax.erf(pre_act * 0.5**0.5))
        slope = (below + pre_act * (jnp.exp(-0.5 * pre_act * pre_act) * (0.5 / jnp.pi) ** 0.5)).astype(bf16)
        hidden = (pre_act * below).astype(bf16)
        pre_grad = dot_nt(grad_all, down_weight) * slope.astype(f32)
        up_bias_part = jnp.sum(pre_grad, axis=0)
        pre_low = pre_grad.astype(bf16)
        back_there = dot_nt(pre_low[own:], up_weight).astype(bf16)
        back_here = dot_nt(pre_low[:own], up_weight)
        second_back = back_here + other(back_there).astype(f32)

        down_there = dot_nn(hidden[own:], down_weight).astype(bf16)
        down_here = dot_nn(hidden[:own], down_weight)
        layer_out = (middle + (down_here + other(down_there).astype(f32)) + down_bias).astype(bf16)
        down_grad = reduce_dp(dot_tn(hidden, grad_all).astype(bf16), order)
        up_grad = reduce_dp(dot_tn(second_low, pre_low).astype(bf16), order)

        def norm_back(back, gain, z, scale):
            scaled = back * gain
            return scale * (
                scaled
                - jnp.mean(scaled, axis=-1, keepdims=True)
                - z * jnp.mean(scaled * z, axis=-1, keepdims=True)
            )

        grad_f = grad_out.astype(f32)
        middle_grad = grad_f + norm_back(second_back, second_gain, second_z, second_scale)
        second_gain_part = jnp.sum(second_back * second_z, axis=0)
        second_shift_part = jnp.sum(second_back, axis=0)
        out_bias_part = jnp.sum(middle_grad, axis=0)
        down_bias_part = jnp.sum(grad_f, axis=0)
        middle_own = middle_grad.astype(bf16)
        middle_all = jnp.concatenate([middle_own, other(middle_own)], axis=0)
        out_grad = reduce_dp(dot_tn(attended, middle_all).astype(bf16), order)
        attended_grad = dot_nt(middle_all, out_weight).astype(bf16)
        dq, dk, dv, query_bias_part, value_bias_part = attend_back(
            qkv, attended_grad, attended, lse, lo, hi, seg_row, seg_col, pairs
        )
        proj_grad = jnp.concatenate([dq, dk, dv], axis=1)
        first_back_part = dot_nt(proj_grad, qkv_flat)
        first_there = first_back_part[own:].astype(bf16)
        first_back = first_back_part[:own] + other(first_there).astype(f32)
        qkv_grad = reduce_dp(dot_tn(first_low, proj_grad).astype(bf16), order)
        first_gain_part = jnp.sum(first_back_part * first_z, axis=0)
        first_shift_part = jnp.sum(first_back_part, axis=0)
        tokens_grad = (
            middle_grad + norm_back(first_back, first_gain, first_z[:own], first_scale[:own])
        ).astype(bf16)
        both = small_sum(
            jnp.stack(
                [
                    first_gain_part, first_shift_part, out_bias_part,
                    second_gain_part, second_shift_part, down_bias_part,
                ]
            ),
            True,
        )
        split = small_sum(
            jnp.concatenate([query_bias_part[0], value_bias_part[0], up_bias_part]).reshape(-1, width),
            False,
        ).reshape(-1)
        return (
            layer_out,
            tokens_grad,
            both[0],
            both[1],
            qkv_grad.astype(f32).reshape(width, 3, local),
            split[:local],
            split[local : 2 * local],
            out_grad.astype(f32),
            both[2],
            both[3],
            both[4],
            up_grad.astype(f32),
            split[2 * local :],
            down_grad.astype(f32),
            both[5],
        )

    return on_device


def solution(mesh):
    rows, whole, tp = P(("dp", "tp"), None), P(), P("tp")
    in_specs = (
        rows, P("dp"), whole, whole, P(None, None, "tp"), tp, tp, P("tp", None),
        whole, whole, whole, P(None, "tp"), tp, P("tp", None), whole, rows,
    )
    out_specs = (
        rows, rows, whole, whole, P(None, None, "tp"), tp, tp, P("tp", None),
        whole, whole, whole, P(None, "tp"), tp, P("tp", None), whole,
    )
    return jax.shard_map(
        make(mesh.shape["dp"]), mesh=mesh, in_specs=in_specs, out_specs=out_specs, check_vma=False
    )
```
